32 devices in a mesh: ta: 4 (over y, x), gx: 2 (over core), gy: 4 (over z).
Axes of the slice: x: 2, y: 2, z: 4, core: 2. Of those that a mesh axis runs over, the one named last changes fastest.
Arguments:
- feat: bfloat16 [4, 2, 4, 768, 128], P('ta', 'gx', 'gy'), may hold values from -6 to 6
- ref_feat: bfloat16 [4, 2, 4, 768, 128], P('ta', 'gx', 'gy'), may hold values from -6 to 6
- rim_rows: int32 [4, 2, 4, 48], P('ta', 'gx', 'gy'), may hold values from 0 to 767
- nbr: int32 [4, 2, 4, 27, 768], P('ta', 'gx', 'gy'), may hold values from 0 to 1200, as said below
- send_blocks: int32 [4, 2, 4, 8, 2], P('ta', 'gx', 'gy'), may hold values from 0 to 5
- send_count: int32 [4, 2, 4, 8], P('ta', 'gx', 'gy'), may hold values from 0 to 2, as said below
- match_slot: int32 [4, 2, 4, 6], P('ta', 'gx', 'gy'), may hold values from 0 to 16, as said below
- labels: int32 [4, 2, 4, 768], P('ta', 'gx', 'gy'), may hold values 0 or 1
- conv_weight: bfloat16 [27, 128, 128], replicated, may hold values from -0.109375 to 0.109375
- ref_weight: bfloat16 [128, 128], replicated, may hold values from -0.5 to 0.5
- cls_weight: bfloat16 [128], replicated, may hold values from -1.796875 to 1.796875
Outputs:
- features_out: bfloat16 [4, 2, 4, 768, 128], P('ta', 'gx', 'gy')
- feature_grad: bfloat16 [4, 2, 4, 768, 128], P('ta', 'gx', 'gy')
- weight_grad: float32 [27, 128, 128], replicated
- ref_grad: float32 [128, 128], replicated
The draws below stay inside these ranges and needn't reach their ends.
Inputs may be any that keep to these rules, and one draw needn't show every extreme that they name: `nbr`: rows index the brick's 768 rows, then the 432 rim rows of the 3 x 3 bricks around it (x outer, own brick in the middle), then the zero row; offset 13 of a voxel is the voxel itself. `send_count`: every brick sends 2 blocks to its own brick, and in each frame one brick drawn from the seed receives 2 blocks from every brick. `match_slot`: 16 means no match; every brick has one or more unmatched blocks.
All inputs are finite; a program needn't handle non-finite values. No bound on the sum of `labels` on one device may be relied on, other than what follows from the above.
Results may differ from the reference program's by a relative error of at most 0.0053.
Values may be sent and summed in bfloat16 or wider, within the bound.
A program may use at most 64 MiB of HBM per device.

```python
import jax
import jax.numpy as jnp
from jax import lax

CHANNELS = 128
OFFSETS = 27
BLOCK = 128
CAP = 2
NB = 6
ROWS = 768
HALO = 48
FRAMES = 4
XBRICKS = 2
YBRICKS = 4
DESTS = 8


def draw_nbr(key, part):
    key_kind, key_local, key_halo = jax.random.split(jax.random.fold_in(key, 11), 3)
    dims = (FRAMES, XBRICKS, YBRICKS, OFFSETS, ROWS)
    choose = jax.random.randint(key_kind, dims, 0, 8)
    local = jax.random.randint(key_local, dims, 0, ROWS)
    remote = ROWS + jax.random.randint(key_halo, dims, 0, 9 * HALO)
    picked = jnp.where(choose == 0, ROWS + 9 * HALO, jnp.where(choose <= 2, remote, local))
    itself = jnp.broadcast_to(jnp.arange(ROWS, dtype=jnp.int32).reshape(1, 1, 1, 1, ROWS), dims)
    offset = jnp.arange(OFFSETS, dtype=jnp.int32).reshape(1, 1, 1, OFFSETS, 1)
    return jnp.where(offset == 13, itself, picked).astype(jnp.int32)


def draw_send_count(key, part):
    key_count, key_hot = jax.random.split(jax.random.fold_in(key, 23))
    counts = jax.random.randint(key_count, (FRAMES, XBRICKS, YBRICKS, DESTS), 0, CAP + 1)
    hottest = jax.random.randint(key_hot, (FRAMES, 1, 1, 1), 0, DESTS)
    own_brick = (jnp.arange(XBRICKS)[:, None] * YBRICKS + jnp.arange(YBRICKS)[None, :])[None, :, :, None]
    target = jnp.arange(DESTS).reshape(1, 1, 1, DESTS)
    return jnp.where((target == own_brick) | (target == hottest), CAP, counts).astype(jnp.int32)


def draw_match_slot(key, part):
    key_slot, key_empty = jax.random.split(jax.random.fold_in(key, 37))
    slots = jax.random.randint(key_slot, (FRAMES, XBRICKS, YBRICKS, NB), 0, DESTS * CAP + 1)
    empty = jax.random.randint(key_empty, (FRAMES, XBRICKS, YBRICKS, 1), 0, NB)
    blocks = jnp.arange(NB).reshape(1, 1, 1, NB)
    return jnp.where(blocks == empty, DESTS * CAP, slots).astype(jnp.int32)


def plant(result, key, low, high):
    shape = result.shape
    place = [jax.random.randint(jax.random.fold_in(key, axis), (), 0, shape[axis]) for axis in range(len(shape))]
    result = result.at[tuple(place)].set(low)
    longest = shape.index(max(shape))
    place[longest] = (place[longest] + 1) % shape[longest]
    return result.at[tuple(place)].set(high)


def level_of(stream_key, extent, cuts, low, top_value):
    gain = 1.0
    for position, shards_of in cuts:
        steps = jax.random.uniform(jax.random.fold_in(jax.random.fold_in(stream_key, 6), position), (shards_of,), jnp.float32, low / len(cuts), top_value / len(cuts))
        gain = gain * jnp.repeat(jnp.exp(steps), extent[position] // shards_of).reshape((-1,) + (1,) * (len(extent) - 1 - position))
    return gain


def noise(own_key, shape, spread, limit, cuts=(), kind=jnp.bfloat16):
    array = spread * jax.random.normal(own_key, shape, jnp.float32)
    if cuts:
        array = array * level_of(own_key, shape, cuts, -0.22, 0.18)
    return jnp.clip(array, -limit, limit).astype(kind)


def setup_inputs(seed: int = 0) -> dict:
    seeds = jax.random.split(jax.random.key(seed), 12)
    return {
        "feat": noise(seeds[0], (FRAMES, XBRICKS, YBRICKS, ROWS, CHANNELS), 1.0, 6.0, ((0, 4), (1, 2), (2, 4))),
        "ref_feat": noise(seeds[1], (FRAMES, XBRICKS, YBRICKS, ROWS, CHANNELS), 1.0, 6.0, ((0, 4), (1, 2), (2, 4))),
        "rim_rows": plant(jax.random.randint(seeds[2], (FRAMES, XBRICKS, YBRICKS, HALO), 0, ROWS), jax.random.fold_in(seeds[2], 1), 0, ROWS - 1).astype(jnp.int32),
        "nbr": draw_nbr(jax.random.fold_in(seeds[11], 71), 0),
        "send_blocks": plant(jax.random.randint(seeds[4], (FRAMES, XBRICKS, YBRICKS, DESTS, CAP), 0, NB), jax.random.fold_in(seeds[4], 1), 0, NB - 1).astype(jnp.int32),
        "send_count": draw_send_count(jax.random.fold_in(seeds[11], 71), 0),
        "match_slot": draw_match_slot(jax.random.fold_in(seeds[11], 71), 0),
        "labels": plant((jax.random.randint(seeds[7], (FRAMES, XBRICKS, YBRICKS, ROWS), 0, 2) < 1).astype(jnp.int32), jax.random.fold_in(seeds[7], 1), 0, 1),
        "conv_weight": noise(seeds[8], (OFFSETS, CHANNELS, CHANNELS), (OFFSETS * CHANNELS) ** -0.5, 0.109375),
        "ref_weight": noise(seeds[9], (CHANNELS, CHANNELS), CHANNELS ** -0.5, 0.5),
        "cls_weight": noise(seeds[10], (CHANNELS,), 0.3, 1.796875),
    }


loss_scale = 16.0


def pick_rows(source, index):
    return source[index]


def add_rows(target, index, values):
    return target.at[index].add(values)


def brick_pass(current, halo_block, matched, offsets_map, label_row, conv_weight, ref_weight, cls_weight):
    channels = current.shape[1]
    extended = jnp.concatenate([current, halo_block.reshape(-1, channels), jnp.zeros((1, channels), current.dtype)], axis=0)

    def forward_step(total, pair):
        index_row, weight = pair
        return total + jnp.dot(extended[index_row], weight, preferred_element_type=jnp.float32), None

    conv_sum = lax.scan(forward_step, jnp.zeros((current.shape[0], channels), jnp.float32), (offsets_map, conv_weight))[0]
    preact = conv_sum + jnp.dot(matched, ref_weight, preferred_element_type=jnp.float32)
    activ = jax.nn.silu(preact).astype(jnp.bfloat16)
    logits = jnp.dot(activ, cls_weight, preferred_element_type=jnp.float32)
    resid = jax.nn.sigmoid(logits) - label_row.astype(jnp.float32)
    sigmas = jax.nn.sigmoid(preact)
    pre_grad = (loss_scale * resid[:, None] * cls_weight.astype(jnp.float32)[None, :] * sigmas * (1.0 + preact * (1.0 - sigmas))).astype(jnp.bfloat16)

    def backward_step(grads, pair):
        index_row, weight = pair
        gathered = extended[index_row]
        weight_term = jnp.dot(gathered.T, pre_grad, preferred_element_type=jnp.float32)
        input_term = jnp.dot(pre_grad, weight.T, preferred_element_type=jnp.float32)
        return grads.at[index_row].add(input_term), weight_term

    ext_grad, weight_terms = lax.scan(backward_step, jnp.zeros((extended.shape[0], channels), jnp.float32), (offsets_map, conv_weight))
    ref_term = jnp.dot(matched.T, pre_grad, preferred_element_type=jnp.float32)
    rows_here = current.shape[0]
    return activ, ext_grad[:rows_here], ext_grad[rows_here:rows_here + halo_block.shape[0] * halo_block.shape[1]], weight_terms, ref_term


def reference(feat, ref_feat, rim_rows, nbr, send_blocks, send_count, match_slot, labels, conv_weight, ref_weight, cls_weight):
    devices_all = FRAMES * XBRICKS * YBRICKS
    rims = jax.vmap(pick_rows)(feat.reshape(devices_all, ROWS, CHANNELS), rim_rows.reshape(devices_all, HALO))
    rims = rims.reshape(FRAMES, XBRICKS, YBRICKS, HALO, CHANNELS)
    padded = jnp.pad(rims, ((0, 0), (1, 1), (1, 1), (0, 0), (0, 0)))
    halos = jnp.stack([padded[:, slot_x:slot_x + XBRICKS, slot_y:slot_y + YBRICKS] for slot_x in range(3) for slot_y in range(3)], axis=3)
    halos = halos.reshape(devices_all, 9, HALO, CHANNELS)

    blocks = ref_feat.reshape(devices_all, NB, BLOCK, CHANNELS)
    lists = send_blocks.reshape(devices_all, DESTS * CAP)
    picked = jax.vmap(pick_rows)(blocks, lists)
    keep = jnp.arange(CAP)[None, None, :] < send_count.reshape(devices_all, DESTS)[:, :, None]
    keep = keep.reshape(devices_all, DESTS * CAP)[:, :, None, None]
    picked = jnp.where(keep, picked, jnp.zeros_like(picked))
    picked = picked.reshape(FRAMES, DESTS, DESTS, CAP, BLOCK, CHANNELS).transpose(0, 2, 1, 3, 4, 5)
    received = jnp.concatenate([jnp.zeros_like(picked[:1]), picked[:-1]], axis=0)
    received = received.reshape(devices_all, DESTS * CAP, BLOCK, CHANNELS)
    table = jnp.concatenate([received, jnp.zeros((devices_all, 1, BLOCK, CHANNELS), received.dtype)], axis=1)
    matched = jax.vmap(pick_rows)(table, match_slot.reshape(devices_all, NB)).reshape(devices_all, ROWS, CHANNELS)

    def per_device(totals, inputs):
        current, halo_block, matched_rows, offsets_map, label_row = inputs
        activ, local_grad, halo_grad, weight_terms, ref_term = brick_pass(current, halo_block, matched_rows, offsets_map, label_row, conv_weight, ref_weight, cls_weight)
        return (totals[0] + weight_terms, totals[1] + ref_term), (activ, local_grad, halo_grad)

    start = (jnp.zeros((OFFSETS, CHANNELS, CHANNELS), jnp.float32), jnp.zeros((CHANNELS, CHANNELS), jnp.float32))
    inputs = (feat.reshape(devices_all, ROWS, CHANNELS), halos, matched, nbr.reshape(devices_all, OFFSETS, ROWS), labels.reshape(devices_all, ROWS))
    totals, outputs = lax.scan(per_device, start, inputs)
    activ, local_grad, halo_grad = outputs
    halo_grad = halo_grad.reshape(FRAMES, XBRICKS, YBRICKS, 3, 3, HALO, CHANNELS)
    halo_pad = jnp.pad(halo_grad, ((0, 0), (1, 1), (1, 1), (0, 0), (0, 0), (0, 0), (0, 0)))
    rim_grad = jnp.zeros((FRAMES, XBRICKS, YBRICKS, HALO, CHANNELS), jnp.float32)
    for slot_x in range(3):
        for slot_y in range(3):
            rim_grad = rim_grad + halo_pad[:, 2 - slot_x:2 - slot_x + XBRICKS, 2 - slot_y:2 - slot_y + YBRICKS, slot_x, slot_y]
    feature_grad = jax.vmap(add_rows)(local_grad, rim_rows.reshape(devices_all, HALO), rim_grad.reshape(devices_all, HALO, CHANNELS))
    shape_out = (FRAMES, XBRICKS, YBRICKS, ROWS, CHANNELS)
    return activ.reshape(shape_out), feature_grad.astype(jnp.bfloat16).reshape(shape_out), totals[0], totals[1]
```

```python
import functools

import jax
import jax.numpy as jnp
from jax import lax
from jax.experimental import pallas as pl
from jax.experimental.pallas import tpu as pltpu
from jax.sharding import PartitionSpec as P

BLOCK = 128
GROUP = 256
MESH = pl.DeviceIdType.MESH

loss_scale = 16.0


def with_halo(block, sides, width):
    for axis, dim in sides:
        count = lax.axis_size(axis)
        forward = [(i, i + 1) for i in range(count - 1)]
        backward = [(target, source) for source, target in forward]
        low = lax.ppermute(
            lax.slice_in_dim(block, block.shape[dim] - width, None, axis=dim), axis, forward
        )
        high = lax.ppermute(lax.slice_in_dim(block, 0, width, axis=dim), axis, backward)
        block = jnp.concatenate([low, block, high], axis=dim)
    return block


def passed_along(block, axis, distance):
    devices = range(lax.axis_size(axis))
    route = [(i - distance, i) for i in devices if i - distance in devices]
    return lax.ppermute(block, axis, route)


def pack_blocks(source, lists, counts):
    channels = source.shape[1]
    blocks = source.reshape(-1, BLOCK, channels)
    picked = blocks[lists]
    keep = jnp.arange(lists.shape[1])[None, :] < counts[:, None]
    return jnp.where(keep[:, :, None, None], picked, jnp.zeros_like(picked))


def route_blocks(buffer):
    return lax.all_to_all(buffer, ("gx", "gy"), split_axis=0, concat_axis=0, tiled=True)


def brick_kernel(
    offsets, groups, ext_ref, matched_ref, nbr_ref, labels_ref, weight_ref, cls_ref,
    activ_ref, own_ref, halo_ref, terms_ref,
    table, onehot, gathered, acc, pgrad,
):
    rows, channels = activ_ref.shape
    center = offsets // 2
    table[...] = jnp.zeros_like(table)
    ext_rows = ext_ref.shape[0]
    for g in range(groups):
        width = min(GROUP, ext_rows - g * GROUP)
        table[pl.ds(g * channels, channels), pl.ds(0, width)] = (
            ext_ref[pl.ds(g * GROUP, width), :].T
        )
    gathered[pl.ds(center * channels, channels), :] = ext_ref[pl.ds(0, rows), :].T
    gathered[pl.ds(offsets * channels, channels), :] = matched_ref[...].T
    slot = lax.broadcasted_iota(jnp.int32, (GROUP, rows), 0)

    def gather_step(j, total):
        o = j + (j >= center).astype(jnp.int32)
        index = nbr_ref[o]
        hit = (slot == (index & (GROUP - 1))).astype(jnp.float32).astype(jnp.bfloat16)
        onehot[o] = hit
        wide = jnp.dot(table[...], hit, preferred_element_type=jnp.float32)
        part = index // GROUP
        picked = wide[:channels]
        for g in range(1, groups):
            picked = jnp.where(part == g, wide[g * channels : (g + 1) * channels], picked)
        picked = picked.astype(jnp.bfloat16)
        gathered[pl.ds(pl.multiple_of(o * channels, channels), channels), :] = picked
        return total + jnp.dot(weight_ref[o].T, picked, preferred_element_type=jnp.float32)

    preact = jnp.zeros((channels, rows), jnp.float32)
    for o in (center, offsets):
        preact += jnp.dot(
            weight_ref[o].T,
            gathered[pl.ds(o * channels, channels), :],
            preferred_element_type=jnp.float32,
        )
    preact = lax.fori_loop(0, offsets - 1, gather_step, preact)
    sigmas = jax.nn.sigmoid(preact)
    activ = (preact * sigmas).astype(jnp.bfloat16)
    activ_ref[...] = activ.T
    scale = cls_ref[...].astype(jnp.float32)
    logits = jnp.sum(activ.astype(jnp.float32) * scale, axis=0, keepdims=True)
    resid = jax.nn.sigmoid(logits) - labels_ref[...].astype(jnp.float32)
    pgrad[...] = (
        loss_scale * resid * scale * sigmas * (1.0 + preact * (1.0 - sigmas))
    ).astype(jnp.bfloat16)

    pad = terms_ref.shape[0] - (offsets + 1) * channels
    if pad:
        terms_ref[pl.ds((offsets + 1) * channels, pad), :] = jnp.zeros((pad, channels), jnp.bfloat16)

    def term_step(o, carry):
        at = pl.ds(pl.multiple_of(o * channels, channels), channels)
        terms_ref[at, :] = lax.dot_general(
            gathered[at, :], pgrad[...], (((1,), (1,)), ((), ())),
            preferred_element_type=jnp.float32,
        ).astype(jnp.bfloat16)
        return carry

    lax.fori_loop(0, offsets + 1, term_step, 0)

    acc[...] = jnp.zeros_like(acc)

    def scatter_step(j, carry):
        o = j + (j >= center).astype(jnp.int32)
        spread = jnp.dot(weight_ref[o], pgrad[...], preferred_element_type=jnp.float32)
        part = nbr_ref[o] // GROUP
        stacked = jnp.concatenate(
            [jnp.where(part == g, spread, 0.0).astype(jnp.bfloat16) for g in range(groups)], axis=0
        )
        acc[...] += lax.dot_general(
            stacked, onehot[o], (((1,), (1,)), ((), ())), preferred_element_type=jnp.float32
        )
        return carry

    lax.fori_loop(0, offsets - 1, scatter_step, 0)
    spread = jnp.dot(weight_ref[center], pgrad[...], preferred_element_type=jnp.float32)
    own_groups = rows // GROUP
    for g in range(own_groups):
        mine = acc[pl.ds(g * channels, channels), :] + spread[:, g * GROUP : (g + 1) * GROUP]
        own_ref[pl.ds(g * GROUP, GROUP), :] = mine.T
    for g in range(own_groups, groups):
        halo_ref[pl.ds((g - own_groups) * GROUP, GROUP), :] = acc[pl.ds(g * channels, channels), :].T


def brick_pass(extended, matched, offsets_map, label_row, weights, cls_weight, term_rows):
    rows, channels = matched.shape
    offsets = offsets_map.shape[0]
    groups = -(-(extended.shape[0] + 1) // GROUP)
    halo_rows = groups * GROUP - rows
    vmem = pl.BlockSpec(memory_space=pltpu.VMEM)
    return pl.pallas_call(
        functools.partial(brick_kernel, offsets, groups),
        out_shape=(
            jax.ShapeDtypeStruct((rows, channels), jnp.bfloat16),
            jax.ShapeDtypeStruct((rows, channels), jnp.float32),
            jax.ShapeDtypeStruct((halo_rows, channels), jnp.float32),
            jax.ShapeDtypeStruct((term_rows, channels), jnp.bfloat16),
        ),
        in_specs=[vmem] * 6,
        out_specs=(vmem,) * 4,
        scratch_shapes=[
            pltpu.VMEM((groups * channels, GROUP), jnp.bfloat16),
            pltpu.VMEM((offsets, GROUP, rows), jnp.bfloat16),
            pltpu.VMEM(((offsets + 1) * channels, rows), jnp.bfloat16),
            pltpu.VMEM((groups * channels, GROUP), jnp.float32),
            pltpu.VMEM((channels, rows), jnp.bfloat16),
        ],
        compiler_params=pltpu.CompilerParams(vmem_limit_bytes=48 * 1024 * 1024),
        name="brick",
    )(
        extended, matched, offsets_map.reshape(offsets, 1, rows), label_row.reshape(1, rows),
        weights, cls_weight.reshape(channels, 1),
    )


AXES = ("gx", "ta", "gy")


def total_kernel(sizes, x_ref, o_ref, *scratch):
    stages = len(AXES)
    recv, part = scratch[:stages], scratch[stages : 2 * stages]
    send_sem, recv_sem, gsend_sem, grecv_sem = scratch[2 * stages : 2 * stages + 4]
    me = [lax.axis_index(axis) for axis in AXES]
    barrier = pltpu.get_barrier_semaphore()
    for i, axis in enumerate(AXES):
        for k in range(1, sizes[i]):
            pl.semaphore_signal(
                barrier, inc=1, device_id={axis: lax.rem(me[i] + k, sizes[i])}, device_id_type=MESH
            )
    pl.semaphore_wait(barrier, sum(sizes) - stages)
    whole = part[-1]
    source = x_ref
    base = 0
    length = x_ref.shape[0]
    bases = []
    slot = 0
    for i, axis in enumerate(AXES):
        n = sizes[i]
        piece = length // n
        copies = []
        for k in range(1, n):
            peer = lax.rem(me[i] + k, n)
            copy = pltpu.make_async_remote_copy(
                src_ref=source.at[pl.ds(pl.multiple_of(peer * piece, 16), piece)],
                dst_ref=recv[i].at[k - 1],
                send_sem=send_sem.at[slot],
                recv_sem=recv_sem.at[slot],
                device_id={axis: peer},
                device_id_type=MESH,
            )
            copy.start()
            copies.append(copy)
            slot += 1
        total = source[pl.ds(pl.multiple_of(me[i] * piece, 16), piece), :].astype(jnp.float32)
        for k, copy in enumerate(copies):
            copy.wait()
            total += recv[i][k].astype(jnp.float32)
        base = base + me[i] * piece
        length = piece
        bases.append((base, piece))
        if i == stages - 1:
            whole[pl.ds(pl.multiple_of(base, 16), piece), :] = total.astype(jnp.bfloat16)
        else:
            part[i][...] = total.astype(jnp.bfloat16)
            source = part[i]
    slot = 0
    for i in reversed(range(stages)):
        n = sizes[i]
        base, piece = bases[i]
        at = whole.at[pl.ds(pl.multiple_of(base, 16), piece)]
        copies = []
        for k in range(1, n):
            copy = pltpu.make_async_remote_copy(
                src_ref=at,
                dst_ref=at,
                send_sem=gsend_sem.at[slot],
                recv_sem=grecv_sem.at[slot],
                device_id={AXES[i]: lax.rem(me[i] + k, n)},
                device_id_type=MESH,
            )
            copy.start()
            copies.append(copy)
            slot += 1
        for copy in copies:
            copy.wait()
    o_ref[...] = whole[...]


def total_terms(terms):
    rows, channels = terms.shape
    sizes = tuple(lax.axis_size(axis) for axis in AXES)
    vmem = pl.BlockSpec(memory_space=pltpu.VMEM)
    recv, part = [], []
    length = rows
    for n in sizes:
        length //= n
        recv.append(pltpu.VMEM((n - 1, length, channels), jnp.bfloat16))
        part.append(pltpu.VMEM((length, channels), jnp.bfloat16))
    part[-1] = pltpu.VMEM((rows, channels), jnp.bfloat16)
    count = sum(sizes) - len(sizes)
    return pl.pallas_call(
        functools.partial(total_kernel, sizes),
        out_shape=jax.ShapeDtypeStruct((rows, channels), jnp.bfloat16),
        in_specs=[vmem],
        out_specs=vmem,
        scratch_shapes=recv + part + [pltpu.SemaphoreType.DMA((count,))] * 4,
        compiler_params=pltpu.CompilerParams(collective_id=0, has_side_effects=True),
        name="total",
    )(terms)


def per_device(
    feat, ref_feat, rim_rows, nbr, send_blocks, send_count, match_slot, labels,
    conv_weight, ref_weight, cls_weight,
):
    current = feat[0, 0, 0]
    rows, channels = current.shape
    offsets = conv_weight.shape[0]
    rim_index = rim_rows[0, 0, 0]
    rim_count = rim_index.shape[0]
    rim_feat = current[rim_index]
    padded = with_halo(rim_feat[None, None, None], (("gx", 1), ("gy", 2)), 1)
    halo_rows = padded[0].reshape(9 * rim_count, channels)
    extended = jnp.concatenate([current, halo_rows], axis=0)
    routed = route_blocks(pack_blocks(ref_feat[0, 0, 0], send_blocks[0, 0, 0], send_count[0, 0, 0]))
    received = passed_along(routed, "ta", 1)
    table = jnp.concatenate(
        [received.reshape(-1, BLOCK, channels), jnp.zeros((1, BLOCK, channels), jnp.bfloat16)],
        axis=0,
    )
    matched = table[match_slot[0, 0, 0]].reshape(rows, channels)
    weights = jnp.concatenate([conv_weight, ref_weight[None]], axis=0)
    devices = lax.axis_size("ta") * lax.axis_size("gx") * lax.axis_size("gy")
    step = 16 * devices
    term_rows = -(-(offsets + 1) * channels // step) * step
    activ, own_grad, halo_grad, terms = brick_pass(
        extended, matched, nbr[0, 0, 0], labels[0, 0, 0], weights, cls_weight, term_rows
    )
    halo_grad = halo_grad[: 9 * rim_count].reshape(3, 3, rim_count, channels)
    column = halo_grad[1]
    for slot_x in (0, 2):
        column = column + passed_along(
            halo_grad[slot_x].astype(jnp.bfloat16), "gx", slot_x - 1
        ).astype(jnp.float32)
    rim_grad = column[1]
    for slot_y in (0, 2):
        rim_grad = rim_grad + passed_along(column[slot_y], "gy", slot_y - 1)
    spot = (jnp.arange(rows)[:, None] == rim_index[None, :]).astype(jnp.bfloat16)
    feature_grad = (
        own_grad
        + jnp.dot(spot, rim_grad.astype(jnp.bfloat16), preferred_element_type=jnp.float32)
    ).astype(jnp.bfloat16)
    summed = total_terms(terms).astype(jnp.float32)
    weight_grad = summed[: offsets * channels].reshape(offsets, channels, channels)
    ref_grad = summed[offsets * channels : (offsets + 1) * channels]
    return (activ[None, None, None], feature_grad[None, None, None], weight_grad, ref_grad)


def solution(mesh):
    placed = (
        P("ta", "gx", "gy", None, None),
        P("ta", "gx", "gy", None, None),
        P("ta", "gx", "gy", None),
        P("ta", "gx", "gy", None, None),
        P("ta", "gx", "gy", None, None),
        P("ta", "gx", "gy", None),
        P("ta", "gx", "gy", None),
        P("ta", "gx", "gy", None),
        P(),
        P(),
        P(),
    )
    return jax.shard_map(
        per_device,
        mesh=mesh,
        in_specs=placed,
        out_specs=(P("ta", "gx", "gy", None, None), P("ta", "gx", "gy", None, None), P(), P()),
        check_vma=False,
    )
```

```python
import functools

import jax
import jax.numpy as jnp
from jax import lax
from jax.experimental import pallas as pl
from jax.experimental.pallas import tpu as pltpu
from jax.sharding import PartitionSpec as P

BLOCK = 128
GROUP = 256
MESH = pl.DeviceIdType.MESH
AXES = ("gx", "ta", "gy")

loss_scale = 16.0


def aligned(start, size):
    return pl.ds(pl.multiple_of(start, 16), size)


def step_kernel(
    sizes, cap, rim_count,
    feat_ref, ref_feat_ref, rim_ref, nbr_ref, lists_ref, counts_ref, match_ref, labels_ref,
    weight_ref, ref_weight_ref, cls_ref,
    activ_ref, fgrad_ref, wsum_ref, rsum_ref,
    table, onehot, gathered, acc, pgrad, terms, rim, rims, outbox, inbox, gbox, gin,
    recv_x, recv_t, recv_y, part_x, part_t, whole,
    rim_send, rim_recv, box_send, box_recv, g_send, g_recv, rs_send, rs_recv, ag_send, ag_recv,
):
    offsets = weight_ref.shape[0]
    rows, channels = feat_ref.shape
    groups = table.shape[0] // channels
    own_groups = rows // GROUP
    center = offsets // 2
    pairs = offsets // 2
    n_x, n_t, n_y = sizes["gx"], sizes["ta"], sizes["gy"]
    bricks = n_x * n_y
    x, t, y = lax.axis_index("gx"), lax.axis_index("ta"), lax.axis_index("gy")
    me = {"gx": x, "ta": t, "gy": y}
    q = x * n_y + y

    around = [(dx, dy) for dx in (-1, 0, 1) for dy in (-1, 0, 1) if (dx, dy) != (0, 0)]

    def inside(dx, dy):
        return (x + dx >= 0) & (x + dx < n_x) & (y + dy >= 0) & (y + dy < n_y)

    def slot_of(dx, dy):
        return (dx + 1) * 3 + dy + 1

    for dx, dy in around:

        @pl.when(jnp.logical_not(inside(dx, dy)))
        def _():
            n = slot_of(dx, dy)
            rims[pl.ds(n * rim_count, rim_count), :] = jnp.zeros((rim_count, channels), jnp.bfloat16)
            gin[n] = jnp.zeros((rim_count, channels), jnp.bfloat16)

    barrier = pltpu.get_barrier_semaphore()
    for axis in AXES:
        for k in range(1, sizes[axis]):
            pl.semaphore_signal(
                barrier, inc=1, device_id={axis: lax.rem(me[axis] + k, sizes[axis])},
                device_id_type=MESH,
            )
    for dx, dy in around:
        if dx and dy:

            @pl.when(inside(dx, dy))
            def _():
                pl.semaphore_signal(
                    barrier, inc=1, device_id={"gx": x + dx, "gy": y + dy}, device_id_type=MESH
                )

    @pl.when(t > 0)
    def _():
        for d in range(bricks):
            pl.semaphore_signal(
                barrier, inc=1, device_id={"ta": t - 1, "gx": d // n_y, "gy": d % n_y},
                device_id_type=MESH,
            )

    spot = (lax.broadcasted_iota(jnp.int32, (rows, rim_count), 0) == rim_ref[...]).astype(
        jnp.float32
    ).astype(jnp.bfloat16)
    mine = lax.dot_general(
        spot, feat_ref[...], (((0,), (0,)), ((), ())), preferred_element_type=jnp.float32
    ).astype(jnp.bfloat16)
    rim[...] = mine
    rims[pl.ds(4 * rim_count, rim_count), :] = mine

    sides_x = (x > 0).astype(jnp.int32) + (x < n_x - 1).astype(jnp.int32)
    sides_y = (y > 0).astype(jnp.int32) + (y < n_y - 1).astype(jnp.int32)
    ahead = (t < n_t - 1).astype(jnp.int32)
    pl.semaphore_wait(barrier, n_x + n_t + n_y - 3 + sides_x * sides_y + ahead * bricks)

    def rim_copy(dx, dy, arriving):
        n = slot_of(dx, dy)
        there = n if arriving else 8 - n
        return pltpu.make_async_remote_copy(
            src_ref=rim,
            dst_ref=rims.at[pl.ds(there * rim_count, rim_count)],
            send_sem=rim_send.at[n],
            recv_sem=rim_recv.at[there],
            device_id={"gx": x + dx, "gy": y + dy},
            device_id_type=MESH,
        )

    for dx, dy in around:

        @pl.when(inside(dx, dy))
        def _():
            rim_copy(dx, dy, False).start()

    def box_copy(k, arriving):
        d = lax.rem(q + k, bricks)
        return pltpu.make_async_remote_copy(
            src_ref=outbox.at[d],
            dst_ref=inbox.at[lax.rem(q + bricks - k, bricks) if arriving else q],
            send_sem=box_send.at[k],
            recv_sem=box_recv.at[k],
            device_id={"ta": lax.rem(t + 1, n_t), "gx": d // n_y, "gy": lax.rem(d, n_y)},
            device_id_type=MESH,
        )

    @pl.when(t < n_t - 1)
    def _():
        for d in range(bricks):
            for s in range(cap):
                block = ref_feat_ref[lists_ref[d * cap + s]]
                outbox[d, s] = jnp.where(s < counts_ref[d], block, jnp.zeros_like(block))
        for k in range(bricks):
            box_copy(k, False).start()

    table[...] = jnp.zeros_like(table)
    for g in range(own_groups):
        table[pl.ds(g * channels, channels), :] = feat_ref[pl.ds(g * GROUP, GROUP), :].T
    gathered[pl.ds(center * channels, channels), :] = feat_ref[...].T

    for dx, dy in around:

        @pl.when(inside(dx, dy))
        def _():
            rim_copy(dx, dy, True).wait_recv()

    halo_rows = 9 * rim_count
    for g in range(own_groups, groups):
        start = (g - own_groups) * GROUP
        width = min(GROUP, halo_rows - start)
        if width > 0:
            table[pl.ds(g * channels, channels), pl.ds(0, width)] = rims[pl.ds(start, width), :].T

    slot = lax.broadcasted_iota(jnp.int32, (GROUP, rows), 0)

    def at(o):
        return pl.ds(pl.multiple_of(o * channels, channels), channels)

    def pick(o):
        index = nbr_ref[pl.ds(o, 1), :]
        hit = (slot == (index & (GROUP - 1))).astype(jnp.float32).astype(jnp.bfloat16)
        onehot[o] = hit
        wide = jnp.dot(table[...], hit, preferred_element_type=jnp.float32)
        part = index // GROUP
        picked = wide[:channels]
        for g in range(1, groups):
            picked = jnp.where(part == g, wide[g * channels : (g + 1) * channels], picked)
        picked = picked.astype(jnp.bfloat16)
        gathered[at(o), :] = picked
        return picked

    def times(first, second, left, right):
        weights = jnp.concatenate([first, second], axis=0)
        return lax.dot_general(
            weights, jnp.concatenate([left, right], axis=0), (((0,), (0,)), ((), ())),
            preferred_element_type=jnp.float32,
        )

    def gather_step(j, total):
        o, p = j, j + center + 1
        return total + times(weight_ref[o], weight_ref[p], pick(o), pick(p))

    preact = lax.fori_loop(0, pairs, gather_step, jnp.zeros((channels, rows), jnp.float32))

    @pl.when(t > 0)
    def _():
        for k in range(bricks):
            box_copy(k, True).wait_recv()

    for k in range(rows // BLOCK):
        where = match_ref[k]
        live = (where < bricks * cap) & (t > 0)
        safe = jnp.minimum(where, bricks * cap - 1)
        block = inbox[safe // cap, lax.rem(safe, cap)]
        block = jnp.where(live, block, jnp.zeros_like(block))
        gathered[pl.ds(offsets * channels, channels), pl.ds(k * BLOCK, BLOCK)] = block.T

    preact += times(
        weight_ref[center], ref_weight_ref[...],
        gathered[pl.ds(center * channels, channels), :],
        gathered[pl.ds(offsets * channels, channels), :],
    )
    sigmas = jax.nn.sigmoid(preact)
    activ = (preact * sigmas).astype(jnp.bfloat16)
    scale = jnp.broadcast_to(cls_ref[...].astype(jnp.float32), (channels, channels)).T[:, :1]
    logits = jnp.sum(activ.astype(jnp.float32) * scale, axis=0, keepdims=True)
    resid = jax.nn.sigmoid(logits) - labels_ref[...].astype(jnp.float32)
    pgrad[...] = (
        loss_scale * resid * scale * sigmas * (1.0 + preact * (1.0 - sigmas))
    ).astype(jnp.bfloat16)

    pad = terms.shape[0] - (offsets + 1) * channels
    if pad:
        terms[pl.ds((offsets + 1) * channels, pad), :] = jnp.zeros((pad, channels), jnp.bfloat16)
    chunk = 4 * channels

    def term_step(j, carry):
        here = pl.ds(pl.multiple_of(j * chunk, chunk), chunk)
        terms[here, :] = lax.dot_general(
            gathered[here, :], pgrad[...], (((1,), (1,)), ((), ())),
            preferred_element_type=jnp.float32,
        ).astype(jnp.bfloat16)
        return carry

    lax.fori_loop(0, (offsets + 1) // 4, term_step, 0)

    recv = {"gx": recv_x, "ta": recv_t, "gy": recv_y}
    source = {"gx": terms, "ta": part_x, "gy": part_t}
    first = {"gx": 0, "ta": n_x - 1, "gy": n_x + n_t - 2}
    piece, base = {}, {}
    length, start = terms.shape[0], 0
    for axis in AXES:
        length //= sizes[axis]
        start = start + me[axis] * length
        piece[axis], base[axis] = length, start

    def rs_copy(axis, k):
        peer = lax.rem(me[axis] + k, sizes[axis])
        return pltpu.make_async_remote_copy(
            src_ref=source[axis].at[aligned(peer * piece[axis], piece[axis])],
            dst_ref=recv[axis].at[k - 1],
            send_sem=rs_send.at[first[axis] + k - 1],
            recv_sem=rs_recv.at[first[axis] + k - 1],
            device_id={axis: peer},
            device_id_type=MESH,
        )

    def rs_start(axis):
        for k in range(1, sizes[axis]):
            rs_copy(axis, k).start()

    def rs_finish(axis):
        total = source[axis][aligned(me[axis] * piece[axis], piece[axis]), :].astype(jnp.float32)
        for k in range(1, sizes[axis]):
            rs_copy(axis, k).wait()
            total += recv[axis][k - 1].astype(jnp.float32)
        return total.astype(jnp.bfloat16)

    def ag_copy(axis, k):
        here = whole.at[aligned(base[axis], piece[axis])]
        return pltpu.make_async_remote_copy(
            src_ref=here,
            dst_ref=here,
            send_sem=ag_send.at[first[axis] + k - 1],
            recv_sem=ag_recv.at[first[axis] + k - 1],
            device_id={axis: lax.rem(me[axis] + k, sizes[axis])},
            device_id_type=MESH,
        )

    def ag_start(axis):
        for k in range(1, sizes[axis]):
            ag_copy(axis, k).start()

    def ag_finish(axis):
        for k in range(1, sizes[axis]):
            ag_copy(axis, k).wait()

    rs_start("gx")
    activ_ref[...] = activ.T
    acc[...] = jnp.zeros_like(acc)

    def scatter_step(j, carry):
        o, p = j, j + center + 1
        spread = jnp.dot(
            jnp.concatenate([weight_ref[o], weight_ref[p]], axis=0), pgrad[...],
            preferred_element_type=jnp.float32,
        )
        total = acc[...]
        for i, n in enumerate((o, p)):
            part = nbr_ref[pl.ds(n, 1), :] // GROUP
            values = spread[i * channels : (i + 1) * channels]
            stacked = jnp.concatenate(
                [jnp.where(part == g, values, 0.0).astype(jnp.bfloat16) for g in range(groups)],
                axis=0,
            )
            total += lax.dot_general(
                stacked, onehot[n], (((1,), (1,)), ((), ())), preferred_element_type=jnp.float32
            )
        acc[...] = total
        return carry

    early, late = pairs // 4, (pairs * 2) // 3
    lax.fori_loop(0, early, scatter_step, 0)
    part_x[...] = rs_finish("gx")
    rs_start("ta")
    lax.fori_loop(early, late, scatter_step, 0)
    part_t[...] = rs_finish("ta")
    rs_start("gy")
    lax.fori_loop(late, pairs, scatter_step, 0)

    for dx in (-1, 0, 1):
        for dy in (-1, 0, 1):
            n = slot_of(dx, dy)
            for g in range(own_groups, groups):
                low = max(n * rim_count, (g - own_groups) * GROUP)
                high = min((n + 1) * rim_count, (g - own_groups + 1) * GROUP)
                if low < high:
                    off = low - (g - own_groups) * GROUP
                    gbox[n, pl.ds(low - n * rim_count, high - low), :] = (
                        acc[pl.ds(g * channels, channels), :].T[off : off + high - low]
                    ).astype(jnp.bfloat16)

    def grad_copy(dx, dy, arriving):
        n = slot_of(dx, dy)
        there = n if arriving else 8 - n
        return pltpu.make_async_remote_copy(
            src_ref=gbox.at[n],
            dst_ref=gin.at[there],
            send_sem=g_send.at[n],
            recv_sem=g_recv.at[there],
            device_id={"gx": x + dx, "gy": y + dy},
            device_id_type=MESH,
        )

    for dx, dy in around:

        @pl.when(inside(dx, dy))
        def _():
            grad_copy(dx, dy, False).start()

    whole[aligned(base["gy"], piece["gy"]), :] = rs_finish("gy")
    ag_start("gy")
    spread = jnp.dot(weight_ref[center], pgrad[...], preferred_element_type=jnp.float32)
    for dx, dy in around:

        @pl.when(inside(dx, dy))
        def _():
            grad_copy(dx, dy, True).wait_recv()

    rim_grad = gbox[4].astype(jnp.float32)
    for dx, dy in around:
        rim_grad += gin[slot_of(dx, dy)].astype(jnp.float32)
    added = jnp.dot(spot, rim_grad.astype(jnp.bfloat16), preferred_element_type=jnp.float32)
    for g in range(own_groups):
        here = slice(g * GROUP, (g + 1) * GROUP)
        own = (acc[pl.ds(g * channels, channels), :] + spread[:, here]).T
        fgrad_ref[pl.ds(g * GROUP, GROUP), :] = (own + added[here]).astype(jnp.bfloat16)
    ag_finish("gy")
    ag_start("ta")
    ag_finish("ta")
    ag_start("gx")
    for dx, dy in around:

        @pl.when(inside(dx, dy))
        def _():
            rim_copy(dx, dy, False).wait_send()
            grad_copy(dx, dy, False).wait_send()

    @pl.when(t < n_t - 1)
    def _():
        for k in range(bricks):
            box_copy(k, False).wait_send()

    ag_finish("gx")
    wsum_ref[...] = whole[pl.ds(0, offsets * channels), :]
    rsum_ref[...] = whole[pl.ds(offsets * channels, channels), :]


def per_device(
    feat, ref_feat, rim_rows, nbr, send_blocks, send_count, match_slot, labels,
    conv_weight, ref_weight, cls_weight,
):
    rows, channels = feat.shape[3:]
    offsets = conv_weight.shape[0]
    bricks, cap = send_blocks.shape[3:]
    rim_count = rim_rows.shape[3]
    sizes = {axis: lax.axis_size(axis) for axis in AXES}
    devices = sizes["ta"] * sizes["gx"] * sizes["gy"]
    step = 16 * devices
    term_rows = -(-(offsets + 1) * channels // step) * step
    groups = -(-(rows + 9 * rim_count + 1) // GROUP)
    vmem = pl.BlockSpec(memory_space=pltpu.VMEM)
    smem = pl.BlockSpec(memory_space=pltpu.SMEM)
    recv, part = [], []
    length = term_rows
    for axis in AXES:
        length //= sizes[axis]
        recv.append(pltpu.VMEM((sizes[axis] - 1, length, channels), jnp.bfloat16))
        part.append(pltpu.VMEM((length, channels), jnp.bfloat16))
    part[-1] = pltpu.VMEM((term_rows, channels), jnp.bfloat16)
    peers = sum(sizes.values()) - 3
    dma = pltpu.SemaphoreType.DMA
    activ, fgrad, wsum, rsum = pl.pallas_call(
        functools.partial(step_kernel, sizes, cap, rim_count),
        out_shape=(
            jax.ShapeDtypeStruct((rows, channels), jnp.bfloat16),
            jax.ShapeDtypeStruct((rows, channels), jnp.bfloat16),
            jax.ShapeDtypeStruct((offsets * channels, channels), jnp.bfloat16),
            jax.ShapeDtypeStruct((channels, channels), jnp.bfloat16),
        ),
        in_specs=[vmem, vmem, vmem, vmem, smem, smem, smem, vmem, vmem, vmem, vmem],
        out_specs=(vmem,) * 4,
        scratch_shapes=[
            pltpu.VMEM((groups * channels, GROUP), jnp.bfloat16),
            pltpu.VMEM((offsets, GROUP, rows), jnp.bfloat16),
            pltpu.VMEM(((offsets + 1) * channels, rows), jnp.bfloat16),
            pltpu.VMEM((groups * channels, GROUP), jnp.float32),
            pltpu.VMEM((channels, rows), jnp.bfloat16),
            pltpu.VMEM((term_rows, channels), jnp.bfloat16),
            pltpu.VMEM((rim_count, channels), jnp.bfloat16),
            pltpu.VMEM((9 * rim_count, channels), jnp.bfloat16),
            pltpu.VMEM((bricks, cap, BLOCK, channels), jnp.bfloat16),
            pltpu.VMEM((bricks, cap, BLOCK, channels), jnp.bfloat16),
            pltpu.VMEM((9, rim_count, channels), jnp.bfloat16),
            pltpu.VMEM((9, rim_count, channels), jnp.bfloat16),
            *recv,
            *part,
            dma((9,)), dma((9,)), dma((bricks,)), dma((bricks,)), dma((9,)), dma((9,)),
            dma((peers,)), dma((peers,)), dma((peers,)), dma((peers,)),
        ],
        compiler_params=pltpu.CompilerParams(
            collective_id=0, has_side_effects=True, vmem_limit_bytes=52 * 1024 * 1024
        ),
        name="step",
    )(
        feat.reshape(rows, channels),
        ref_feat.reshape(rows // BLOCK, BLOCK, channels),
        rim_rows.reshape(1, rim_count),
        nbr.reshape(offsets, rows),
        send_blocks.reshape(bricks * cap),
        send_count.reshape(bricks),
        match_slot.reshape(rows // BLOCK),
        labels.reshape(1, rows),
        conv_weight,
        ref_weight,
        cls_weight.reshape(1, channels),
    )
    whole = (1, 1, 1, rows, channels)
    weight_grad = wsum.astype(jnp.float32).reshape(offsets, channels, channels)
    return activ.reshape(whole), fgrad.reshape(whole), weight_grad, rsum.astype(jnp.float32)


def solution(mesh):
    placed = (
        P("ta", "gx", "gy", None, None),
        P("ta", "gx", "gy", None, None),
        P("ta", "gx", "gy", None),
        P("ta", "gx", "gy", None, None),
        P("ta", "gx", "gy", None, None),
        P("ta", "gx", "gy", None),
        P("ta", "gx", "gy", None),
        P("ta", "gx", "gy", None),
        P(),
        P(),
        P(),
    )
    return jax.shard_map(
        per_device,
        mesh=mesh,
        in_specs=placed,
        out_specs=(P("ta", "gx", "gy", None, None), P("ta", "gx", "gy", None, None), P(), P()),
        check_vma=False,
    )
```

```python
import functools

import jax
import jax.numpy as jnp
from jax import lax
from jax.experimental import pallas as pl
from jax.experimental.pallas import tpu as pltpu
from jax.sharding import PartitionSpec as P

BLOCK = 128
GROUP = 256
MESH = pl.DeviceIdType.MESH
AXES = ("gx", "ta", "gy")

loss_scale = 16.0


def aligned(start, size):
    return pl.ds(pl.multiple_of(start, 16), size)


def step_kernel(
    sizes, cap, rim_count,
    feat_hbm, ref_feat_hbm, rim_hbm, nbr_hbm, lists_hbm, counts_hbm, match_hbm, labels_hbm,
    weight_hbm, ref_weight_hbm, cls_hbm,
    activ_ref, fgrad_ref, wsum_ref, rsum_ref,
    table, onehot, gathered, acc, pgrad, terms, rim, rims, outbox, inbox, gbox, gin,
    recv_x, recv_t, recv_y, part_x, part_t, whole,
    feat_ref, ref_feat_ref, rim_ref, nbr_ref, lists_ref, counts_ref, match_ref, labels_ref,
    weight_ref, ref_weight_ref, cls_ref, load_sem,
    rim_send, rim_recv, box_send, box_recv, g_send, g_recv, rs_send, rs_recv, ag_send, ag_recv,
):
    offsets = weight_ref.shape[0]
    rows, channels = feat_ref.shape
    loads = [
        pltpu.make_async_copy(src, dst, load_sem.at[i])
        for i, (src, dst) in enumerate((
            (feat_hbm, feat_ref), (rim_hbm, rim_ref), (ref_feat_hbm, ref_feat_ref),
            (lists_hbm, lists_ref), (counts_hbm, counts_ref), (nbr_hbm, nbr_ref),
            (weight_hbm, weight_ref), (ref_weight_hbm, ref_weight_ref), (match_hbm, match_ref),
            (labels_hbm, labels_ref), (cls_hbm, cls_ref),
        ))
    ]
    for load in loads:
        load.start()
    groups = table.shape[0] // channels
    own_groups = rows // GROUP
    center = offsets // 2
    pairs = offsets // 2
    n_x, n_t, n_y = sizes["gx"], sizes["ta"], sizes["gy"]
    bricks = n_x * n_y
    x, t, y = lax.axis_index("gx"), lax.axis_index("ta"), lax.axis_index("gy")
    me = {"gx": x, "ta": t, "gy": y}
    q = x * n_y + y

    around = [(dx, dy) for dx in (-1, 0, 1) for dy in (-1, 0, 1) if (dx, dy) != (0, 0)]

    def inside(dx, dy):
        return (x + dx >= 0) & (x + dx < n_x) & (y + dy >= 0) & (y + dy < n_y)

    def slot_of(dx, dy):
        return (dx + 1) * 3 + dy + 1

    for dx, dy in around:

        @pl.when(jnp.logical_not(inside(dx, dy)))
        def _():
            n = slot_of(dx, dy)
            rims[pl.ds(n * rim_count, rim_count), :] = jnp.zeros((rim_count, channels), jnp.bfloat16)
            gin[n] = jnp.zeros((rim_count, channels), jnp.bfloat16)

    barrier = pltpu.get_barrier_semaphore()
    for axis in AXES:
        for k in range(1, sizes[axis]):
            pl.semaphore_signal(
                barrier, inc=1, device_id={axis: lax.rem(me[axis] + k, sizes[axis])},
                device_id_type=MESH,
            )
    for dx, dy in around:
        if dx and dy:

            @pl.when(inside(dx, dy))
            def _():
                pl.semaphore_signal(
                    barrier, inc=1, device_id={"gx": x + dx, "gy": y + dy}, device_id_type=MESH
                )

    @pl.when(t > 0)
    def _():
        for d in range(bricks):
            pl.semaphore_signal(
                barrier, inc=1, device_id={"ta": t - 1, "gx": d // n_y, "gy": d % n_y},
                device_id_type=MESH,
            )

    loads[0].wait()
    loads[1].wait()
    spot = (lax.broadcasted_iota(jnp.int32, (rows, rim_count), 0) == rim_ref[...]).astype(
        jnp.float32
    ).astype(jnp.bfloat16)
    mine = lax.dot_general(
        spot, feat_ref[...], (((0,), (0,)), ((), ())), preferred_element_type=jnp.float32
    ).astype(jnp.bfloat16)
    rim[...] = mine
    rims[pl.ds(4 * rim_count, rim_count), :] = mine

    sides_x = (x > 0).astype(jnp.int32) + (x < n_x - 1).astype(jnp.int32)
    sides_y = (y > 0).astype(jnp.int32) + (y < n_y - 1).astype(jnp.int32)
    ahead = (t < n_t - 1).astype(jnp.int32)
    pl.semaphore_wait(barrier, n_x + n_t + n_y - 3 + sides_x * sides_y + ahead * bricks)

    def rim_copy(dx, dy, arriving):
        n = slot_of(dx, dy)
        there = n if arriving else 8 - n
        return pltpu.make_async_remote_copy(
            src_ref=rim,
            dst_ref=rims.at[pl.ds(there * rim_count, rim_count)],
            send_sem=rim_send.at[n],
            recv_sem=rim_recv.at[there],
            device_id={"gx": x + dx, "gy": y + dy},
            device_id_type=MESH,
        )

    for dx, dy in around:

        @pl.when(inside(dx, dy))
        def _():
            rim_copy(dx, dy, False).start()

    def box_copy(k, arriving):
        d = lax.rem(q + k, bricks)
        return pltpu.make_async_remote_copy(
            src_ref=outbox.at[d],
            dst_ref=inbox.at[lax.rem(q + bricks - k, bricks) if arriving else q],
            send_sem=box_send.at[k],
            recv_sem=box_recv.at[k],
            device_id={"ta": lax.rem(t + 1, n_t), "gx": d // n_y, "gy": lax.rem(d, n_y)},
            device_id_type=MESH,
        )

    for load in loads[2:]:
        load.wait()

    @pl.when(t < n_t - 1)
    def _():
        for d in range(bricks):
            for s in range(cap):
                block = ref_feat_ref[lists_ref[d, s]]
                outbox[d, s] = jnp.where(s < counts_ref[0, d], block, jnp.zeros_like(block))
        for k in range(bricks):
            box_copy(k, False).start()

    table[...] = jnp.zeros_like(table)
    for g in range(own_groups):
        table[pl.ds(g * channels, channels), :] = feat_ref[pl.ds(g * GROUP, GROUP), :].T
    gathered[pl.ds(center * channels, channels), :] = feat_ref[...].T

    for dx, dy in around:

        @pl.when(inside(dx, dy))
        def _():
            rim_copy(dx, dy, True).wait_recv()

    halo_rows = 9 * rim_count
    for g in range(own_groups, groups):
        start = (g - own_groups) * GROUP
        width = min(GROUP, halo_rows - start)
        if width > 0:
            table[pl.ds(g * channels, channels), pl.ds(0, width)] = rims[pl.ds(start, width), :].T

    slot = lax.broadcasted_iota(jnp.int32, (GROUP, rows), 0)

    def at(o):
        return pl.ds(pl.multiple_of(o * channels, channels), channels)

    def pick(o):
        index = nbr_ref[pl.ds(o, 1), :]
        hit = (slot == (index & (GROUP - 1))).astype(jnp.float32).astype(jnp.bfloat16)
        onehot[o] = hit
        wide = jnp.dot(table[...], hit, preferred_element_type=jnp.float32)
        part = index // GROUP
        picked = wide[:channels]
        for g in range(1, groups):
            picked = jnp.where(part == g, wide[g * channels : (g + 1) * channels], picked)
        picked = picked.astype(jnp.bfloat16)
        gathered[at(o), :] = picked
        return picked

    def times(first, second, left, right):
        weights = jnp.concatenate([first, second], axis=0)
        return lax.dot_general(
            weights, jnp.concatenate([left, right], axis=0), (((0,), (0,)), ((), ())),
            preferred_element_type=jnp.float32,
        )

    def gather_step(j, total):
        o, p = j, j + center + 1
        return total + times(weight_ref[o], weight_ref[p], pick(o), pick(p))

    preact = lax.fori_loop(0, pairs, gather_step, jnp.zeros((channels, rows), jnp.float32))

    @pl.when(t > 0)
    def _():
        for k in range(bricks):
            box_copy(k, True).wait_recv()

    for k in range(rows // BLOCK):
        where = match_ref[0, k]
        live = (where < bricks * cap) & (t > 0)
        safe = jnp.minimum(where, bricks * cap - 1)
        block = inbox[safe // cap, lax.rem(safe, cap)]
        block = jnp.where(live, block, jnp.zeros_like(block))
        gathered[pl.ds(offsets * channels, channels), pl.ds(k * BLOCK, BLOCK)] = block.T

    preact += times(
        weight_ref[center], ref_weight_ref[...],
        gathered[pl.ds(center * channels, channels), :],
        gathered[pl.ds(offsets * channels, channels), :],
    )
    sigmas = jax.nn.sigmoid(preact)
    activ = (preact * sigmas).astype(jnp.bfloat16)
    scale = jnp.broadcast_to(cls_ref[...].astype(jnp.float32), (channels, channels)).T[:, :1]
    logits = jnp.sum(activ.astype(jnp.float32) * scale, axis=0, keepdims=True)
    resid = jax.nn.sigmoid(logits) - labels_ref[...].astype(jnp.float32)
    pgrad[...] = (
        loss_scale * resid * scale * sigmas * (1.0 + preact * (1.0 - sigmas))
    ).astype(jnp.bfloat16)

    pad = terms.shape[0] - (offsets + 1) * channels
    if pad:
        terms[pl.ds((offsets + 1) * channels, pad), :] = jnp.zeros((pad, channels), jnp.bfloat16)
    chunk = 4 * channels

    def term_step(j, carry):
        here = pl.ds(pl.multiple_of(j * chunk, chunk), chunk)
        terms[here, :] = lax.dot_general(
            gathered[here, :], pgrad[...], (((1,), (1,)), ((), ())),
            preferred_element_type=jnp.float32,
        ).astype(jnp.bfloat16)
        return carry

    lax.fori_loop(0, (offsets + 1) // 4, term_step, 0)

    recv = {"gx": recv_x, "ta": recv_t, "gy": recv_y}
    source = {"gx": terms, "ta": part_x, "gy": part_t}
    first = {"gx": 0, "ta": n_x - 1, "gy": n_x + n_t - 2}
    piece, base = {}, {}
    length, start = terms.shape[0], 0
    for axis in AXES:
        length //= sizes[axis]
        start = start + me[axis] * length
        piece[axis], base[axis] = length, start

    def rs_copy(axis, k):
        peer = lax.rem(me[axis] + k, sizes[axis])
        return pltpu.make_async_remote_copy(
            src_ref=source[axis].at[aligned(peer * piece[axis], piece[axis])],
            dst_ref=recv[axis].at[k - 1],
            send_sem=rs_send.at[first[axis] + k - 1],
            recv_sem=rs_recv.at[first[axis] + k - 1],
            device_id={axis: peer},
            device_id_type=MESH,
        )

    def rs_start(axis):
        for k in range(1, sizes[axis]):
            rs_copy(axis, k).start()

    def rs_finish(axis):
        total = source[axis][aligned(me[axis] * piece[axis], piece[axis]), :].astype(jnp.float32)
        for k in range(1, sizes[axis]):
            rs_copy(axis, k).wait()
            total += recv[axis][k - 1].astype(jnp.float32)
        return total.astype(jnp.bfloat16)

    def ag_copy(axis, k):
        here = whole.at[aligned(base[axis], piece[axis])]
        return pltpu.make_async_remote_copy(
            src_ref=here,
            dst_ref=here,
            send_sem=ag_send.at[first[axis] + k - 1],
            recv_sem=ag_recv.at[first[axis] + k - 1],
            device_id={axis: lax.rem(me[axis] + k, sizes[axis])},
            device_id_type=MESH,
        )

    def ag_start(axis):
        for k in range(1, sizes[axis]):
            ag_copy(axis, k).start()

    def ag_finish(axis):
        for k in range(1, sizes[axis]):
            ag_copy(axis, k).wait()

    rs_start("gx")
    activ_ref[...] = activ.T
    acc[...] = jnp.zeros_like(acc)

    def scatter_step(j, carry):
        o, p = j, j + center + 1
        spread = jnp.dot(
            jnp.concatenate([weight_ref[o], weight_ref[p]], axis=0), pgrad[...],
            preferred_element_type=jnp.float32,
        )
        total = acc[...]
        for i, n in enumerate((o, p)):
            part = nbr_ref[pl.ds(n, 1), :] // GROUP
            values = spread[i * channels : (i + 1) * channels]
            stacked = jnp.concatenate(
                [jnp.where(part == g, values, 0.0).astype(jnp.bfloat16) for g in range(groups)],
                axis=0,
            )
            total += lax.dot_general(
                stacked, onehot[n], (((1,), (1,)), ((), ())), preferred_element_type=jnp.float32
            )
        acc[...] = total
        return carry

    early, late = pairs // 4, (pairs * 2) // 3
    lax.fori_loop(0, early, scatter_step, 0)
    part_x[...] = rs_finish("gx")
    rs_start("ta")
    lax.fori_loop(early, late, scatter_step, 0)
    part_t[...] = rs_finish("ta")
    rs_start("gy")
    lax.fori_loop(late, pairs, scatter_step, 0)

    for dx in (-1, 0, 1):
        for dy in (-1, 0, 1):
            n = slot_of(dx, dy)
            for g in range(own_groups, groups):
                low = max(n * rim_count, (g - own_groups) * GROUP)
                high = min((n + 1) * rim_count, (g - own_groups + 1) * GROUP)
                if low < high:
                    off = low - (g - own_groups) * GROUP
                    gbox[n, pl.ds(low - n * rim_count, high - low), :] = (
                        acc[pl.ds(g * channels, channels), :].T[off : off + high - low]
                    ).astype(jnp.bfloat16)

    def grad_copy(dx, dy, arriving):
        n = slot_of(dx, dy)
        there = n if arriving else 8 - n
        return pltpu.make_async_remote_copy(
            src_ref=gbox.at[n],
            dst_ref=gin.at[there],
            send_sem=g_send.at[n],
            recv_sem=g_recv.at[there],
            device_id={"gx": x + dx, "gy": y + dy},
            device_id_type=MESH,
        )

    for dx, dy in around:

        @pl.when(inside(dx, dy))
        def _():
            grad_copy(dx, dy, False).start()

    whole[aligned(base["gy"], piece["gy"]), :] = rs_finish("gy")
    ag_start("gy")
    spread = jnp.dot(weight_ref[center], pgrad[...], preferred_element_type=jnp.float32)
    for dx, dy in around:

        @pl.when(inside(dx, dy))
        def _():
            grad_copy(dx, dy, True).wait_recv()

    rim_grad = gbox[4].astype(jnp.float32)
    for dx, dy in around:
        rim_grad += gin[slot_of(dx, dy)].astype(jnp.float32)
    added = jnp.dot(spot, rim_grad.astype(jnp.bfloat16), preferred_element_type=jnp.float32)
    for g in range(own_groups):
        here = slice(g * GROUP, (g + 1) * GROUP)
        own = (acc[pl.ds(g * channels, channels), :] + spread[:, here]).T
        fgrad_ref[pl.ds(g * GROUP, GROUP), :] = (own + added[here]).astype(jnp.bfloat16)
    ag_finish("gy")
    ag_start("ta")
    ag_finish("ta")
    ag_start("gx")
    for dx, dy in around:

        @pl.when(inside(dx, dy))
        def _():
            rim_copy(dx, dy, False).wait_send()
            grad_copy(dx, dy, False).wait_send()

    @pl.when(t < n_t - 1)
    def _():
        for k in range(bricks):
            box_copy(k, False).wait_send()

    ag_finish("gx")
    wsum_ref[...] = whole[pl.ds(0, offsets * channels), :]
    rsum_ref[...] = whole[pl.ds(offsets * channels, channels), :]


def finish_kernel(activ_ref, fgrad_ref, wsum_ref, rsum_ref, activ_out, fgrad_out, wsum_out, rsum_out):
    activ_out[...] = activ_ref[...]
    fgrad_out[...] = fgrad_ref[...]
    wsum_out[...] = wsum_ref[...].astype(jnp.float32)
    rsum_out[...] = rsum_ref[...].astype(jnp.float32)


def per_device(
    feat, ref_feat, rim_rows, nbr, send_blocks, send_count, match_slot, labels,
    conv_weight, ref_weight, cls_weight,
):
    rows, channels = feat.shape[3:]
    offsets = conv_weight.shape[0]
    bricks, cap = send_blocks.shape[3:]
    rim_count = rim_rows.shape[3]
    sizes = {axis: lax.axis_size(axis) for axis in AXES}
    devices = sizes["ta"] * sizes["gx"] * sizes["gy"]
    step = 16 * devices
    term_rows = -(-(offsets + 1) * channels // step) * step
    groups = -(-(rows + 9 * rim_count + 1) // GROUP)
    vmem = pl.BlockSpec(memory_space=pltpu.VMEM)
    recv, part = [], []
    length = term_rows
    for axis in AXES:
        length //= sizes[axis]
        recv.append(pltpu.VMEM((sizes[axis] - 1, length, channels), jnp.bfloat16))
        part.append(pltpu.VMEM((length, channels), jnp.bfloat16))
    part[-1] = pltpu.VMEM((term_rows, channels), jnp.bfloat16)
    peers = sum(sizes.values()) - 3
    dma = pltpu.SemaphoreType.DMA
    activ, fgrad, wsum, rsum = pl.pallas_call(
        functools.partial(step_kernel, sizes, cap, rim_count),
        out_shape=(
            jax.ShapeDtypeStruct((rows, channels), jnp.bfloat16),
            jax.ShapeDtypeStruct((rows, channels), jnp.bfloat16),
            jax.ShapeDtypeStruct((offsets * channels, channels), jnp.bfloat16),
            jax.ShapeDtypeStruct((channels, channels), jnp.bfloat16),
        ),
        in_specs=[pl.BlockSpec(memory_space=pltpu.HBM)] * 11,
        out_specs=(vmem,) * 4,
        scratch_shapes=[
            pltpu.VMEM((groups * channels, GROUP), jnp.bfloat16),
            pltpu.VMEM((offsets, GROUP, rows), jnp.bfloat16),
            pltpu.VMEM(((offsets + 1) * channels, rows), jnp.bfloat16),
            pltpu.VMEM((groups * channels, GROUP), jnp.float32),
            pltpu.VMEM((channels, rows), jnp.bfloat16),
            pltpu.VMEM((term_rows, channels), jnp.bfloat16),
            pltpu.VMEM((rim_count, channels), jnp.bfloat16),
            pltpu.VMEM((9 * rim_count, channels), jnp.bfloat16),
            pltpu.VMEM((bricks, cap, BLOCK, channels), jnp.bfloat16),
            pltpu.VMEM((bricks, cap, BLOCK, channels), jnp.bfloat16),
            pltpu.VMEM((9, rim_count, channels), jnp.bfloat16),
            pltpu.VMEM((9, rim_count, channels), jnp.bfloat16),
            *recv,
            *part,
            pltpu.VMEM((rows, channels), jnp.bfloat16),
            pltpu.VMEM((rows // BLOCK, BLOCK, channels), jnp.bfloat16),
            pltpu.VMEM((1, rim_count), jnp.int32),
            pltpu.VMEM((offsets, rows), jnp.int32),
            pltpu.SMEM((bricks, cap), jnp.int32),
            pltpu.SMEM((1, bricks), jnp.int32),
            pltpu.SMEM((1, rows // BLOCK), jnp.int32),
            pltpu.VMEM((1, rows), jnp.int32),
            pltpu.VMEM((offsets, channels, channels), jnp.bfloat16),
            pltpu.VMEM((channels, channels), jnp.bfloat16),
            pltpu.VMEM((1, channels), jnp.bfloat16),
            dma((11,)),
            dma((9,)), dma((9,)), dma((bricks,)), dma((bricks,)), dma((9,)), dma((9,)),
            dma((peers,)), dma((peers,)), dma((peers,)), dma((peers,)),
        ],
        compiler_params=pltpu.CompilerParams(
            collective_id=0, has_side_effects=True, vmem_limit_bytes=60 * 1024 * 1024
        ),
        name="step",
    )(
        feat.reshape(rows, channels),
        ref_feat.reshape(rows // BLOCK, BLOCK, channels),
        rim_rows.reshape(1, rim_count),
        nbr.reshape(offsets, rows),
        send_blocks.reshape(bricks, cap),
        send_count.reshape(1, bricks),
        match_slot.reshape(1, rows // BLOCK),
        labels.reshape(1, rows),
        conv_weight,
        ref_weight,
        cls_weight.reshape(1, channels),
    )
    activ, fgrad, wsum, rsum = pl.pallas_call(
        finish_kernel,
        out_shape=(
            jax.ShapeDtypeStruct((rows, channels), jnp.bfloat16),
            jax.ShapeDtypeStruct((rows, channels), jnp.bfloat16),
            jax.ShapeDtypeStruct((offsets * channels, channels), jnp.float32),
            jax.ShapeDtypeStruct((channels, channels), jnp.float32),
        ),
        in_specs=[vmem] * 4,
        out_specs=(vmem,) * 4,
        name="finish",
    )(activ, fgrad, wsum, rsum)
    whole = (1, 1, 1, rows, channels)
    weight_grad = wsum.reshape(offsets, channels, channels)
    return activ.reshape(whole), fgrad.reshape(whole), weight_grad, rsum


def solution(mesh):
    placed = (
        P("ta", "gx", "gy", None, None),
        P("ta", "gx", "gy", None, None),
        P("ta", "gx", "gy", None),
        P("ta", "gx", "gy", None, None),
        P("ta", "gx", "gy", None, None),
        P("ta", "gx", "gy", None),
        P("ta", "gx", "gy", None),
        P("ta", "gx", "gy", None),
        P(),
        P(),
        P(),
    )
    return jax.shard_map(
        per_device,
        mesh=mesh,
        in_specs=placed,
        out_specs=(P("ta", "gx", "gy", None, None), P("ta", "gx", "gy", None, None), P(), P()),
        check_vma=False,
    )
```
